32 devices in a mesh: gy: 4 (over y, x), gz: 8 (over z, core).
Axes of the slice: x: 2, y: 2, z: 4, core: 2. Of those that a mesh axis runs over, the one named last changes fastest.
Arguments:
- conduct: float32 [64, 256, 128], P('gy', 'gz'), may hold values from 0.3 to 3
- seeds: int32 [64, 256, 128], P('gy', 'gz'), may hold values 0 or 1
- labels: int32 [64, 256, 128], P('gy', 'gz'), may hold values 0 or 1
- start: float32 [64, 256, 128], P('gy', 'gz'), may hold values from 0 to 1
- cotangent: float32 [64, 256, 128], P('gy', 'gz'), may hold values from -12 to 12
Outputs:
- probability: float32 [64, 256, 128], P('gy', 'gz')
- adjoint: float32 [64, 256, 128], P('gy', 'gz')
- grad_conduct: float32 [64, 256, 128], P('gy', 'gz')
The draws below stay inside these ranges and needn't reach their ends.
All inputs are finite; a program needn't handle non-finite values. No bound on the sum of `seeds` or of `labels` on one device may be relied on, other than what follows from the above.
Results may differ from the reference program's by a relative error of at most 0.0001.
Values sent between devices are 32-bit elements; how exact they have to be, the bound alone decides.
A program may use at most 64 MiB of HBM per device.

```python
import math
import jax
import jax.numpy as jnp

NX = 128
ITERS = 2
NY = 64
NZ = 256


def draw_cotangent(key, part):
    rows = jnp.arange(NY, dtype=jnp.float32) / max(NY - 1, 1)
    values = jnp.clip(jax.random.normal(key, (NY, NZ, NX), jnp.float32), -4.0, 4.0)
    return values * (1.0 + 2.0 * rows)[:, None, None]


def plant(array, key, least, top_value):
    longest = array.shape.index(max(array.shape))
    spots = []
    for shift in (0, 1):
        where = [jax.random.randint(jax.random.fold_in(key, axis), (), 0, length) for axis, length in enumerate(array.shape)]
        where[longest] = (where[longest] + shift) % array.shape[longest]
        spots.append(tuple(where))
    return array.at[spots[0]].set(least).at[spots[1]].set(top_value)


def level_of(rng, extent, cuts, least, top_value):
    factor_of = 1.0
    for dim, blocks in cuts:
        heights = jax.random.uniform(jax.random.fold_in(jax.random.fold_in(rng, 6), dim), (blocks,), jnp.float32, least / len(cuts), top_value / len(cuts))
        factor_of = factor_of * jnp.repeat(jnp.exp(heights), extent[dim] // blocks).reshape((-1,) + (1,) * (len(extent) - 1 - dim))
    return factor_of


def setup_inputs(seed: int = 0) -> dict:
    streams_of = jax.random.split(jax.random.key(seed), 6)
    return {
        "conduct": jnp.clip(jnp.exp(math.log(3.0) - 2.3025851 * jax.random.uniform(streams_of[0], (NY, NZ, NX), jnp.float32) ** level_of(streams_of[0], (NY, NZ, NX), ((0, 4), (1, 8)), -0.2, 0.2)), 0.3, 3.0),
        "seeds": plant((jax.random.randint(streams_of[1], (NY, NZ, NX), 0, 8) < 1).astype(jnp.int32), jax.random.fold_in(streams_of[1], 1), 0, 1),
        "labels": plant((jax.random.randint(streams_of[2], (NY, NZ, NX), 0, 2) < 1).astype(jnp.int32), jax.random.fold_in(streams_of[2], 1), 0, 1),
        "start": jnp.clip(1.0 * jax.random.uniform(streams_of[3], (NY, NZ, NX), jnp.float32) ** level_of(streams_of[3], (NY, NZ, NX), ((0, 4), (1, 8)), -0.2, 0.2), 0.0, 1.0),
        "cotangent": draw_cotangent(jax.random.fold_in(streams_of[5], 71), 0),
    }


seed_pull = 4.0
screening = 0.05


def harmonic(first, second):
    return 2.0 * first * second / (first + second)


def pad_sides(field):
    return jnp.pad(field, ((1, 1), (1, 1), (0, 0)))


def coefficients(padded_cond, seeds):
    core = padded_cond[1:-1, 1:-1]
    along = jnp.pad(core, ((0, 0), (0, 0), (1, 1)))
    weights = (harmonic(core, padded_cond[2:, 1:-1]), harmonic(core, padded_cond[:-2, 1:-1]),
               harmonic(core, padded_cond[1:-1, 2:]), harmonic(core, padded_cond[1:-1, :-2]),
               harmonic(core, along[..., 2:]), harmonic(core, along[..., :-2]))
    diagonal = weights[0] + weights[1] + weights[2] + weights[3] + weights[4] + weights[5]
    diagonal = diagonal + seed_pull * seeds.astype(jnp.float32) + screening
    return (diagonal,) + weights


def operate(padded, coeffs):
    field = padded[1:-1, 1:-1]
    along = jnp.pad(field, ((0, 0), (0, 0), (1, 1)))
    out = coeffs[0] * field - coeffs[1] * padded[2:, 1:-1] - coeffs[2] * padded[:-2, 1:-1]
    out = out - coeffs[3] * padded[1:-1, 2:] - coeffs[4] * padded[1:-1, :-2]
    return out - coeffs[5] * along[..., 2:] - coeffs[6] * along[..., :-2]


def edge_term(ci, cj, ui, uj, vi, vj):
    total = ci + cj
    return -2.0 * cj * cj / (total * total) * (ui - uj) * (vi - vj)


def gradient(cond_pad, prob_pad, adj_pad):
    ci = cond_pad[1:-1, 1:-1]
    ui = prob_pad[1:-1, 1:-1]
    vi = adj_pad[1:-1, 1:-1]
    out = edge_term(ci, cond_pad[2:, 1:-1], ui, prob_pad[2:, 1:-1], vi, adj_pad[2:, 1:-1])
    out = out + edge_term(ci, cond_pad[:-2, 1:-1], ui, prob_pad[:-2, 1:-1], vi, adj_pad[:-2, 1:-1])
    out = out + edge_term(ci, cond_pad[1:-1, 2:], ui, prob_pad[1:-1, 2:], vi, adj_pad[1:-1, 2:])
    out = out + edge_term(ci, cond_pad[1:-1, :-2], ui, prob_pad[1:-1, :-2], vi, adj_pad[1:-1, :-2])
    cx = jnp.pad(ci, ((0, 0), (0, 0), (1, 1)))
    ux = jnp.pad(ui, ((0, 0), (0, 0), (1, 1)))
    vx = jnp.pad(vi, ((0, 0), (0, 0), (1, 1)))
    out = out + edge_term(ci, cx[..., 2:], ui, ux[..., 2:], vi, vx[..., 2:])
    return out + edge_term(ci, cx[..., :-2], ui, ux[..., :-2], vi, vx[..., :-2])


def conjugate(iterate, resid, coeffs):
    direction = resid
    norm_now = jnp.sum(resid * resid)
    for step in range(ITERS):
        image = operate(pad_sides(direction), coeffs)
        alpha = norm_now / jnp.sum(direction * image)
        iterate = iterate + alpha * direction
        resid = resid - alpha * image
        norm_next = jnp.sum(resid * resid)
        direction = resid + (norm_next / norm_now) * direction
        norm_now = norm_next
    return iterate


def reference(conduct, seeds, labels, start, cotangent):
    cond_pad = pad_sides(conduct)
    coeffs = coefficients(cond_pad, seeds)
    rhs = seed_pull * (seeds * labels).astype(jnp.float32)
    probability = conjugate(start, rhs - operate(pad_sides(start), coeffs), coeffs)
    adjoint = conjugate(jnp.zeros_like(cotangent), cotangent, coeffs)
    grad_conduct = gradient(cond_pad, pad_sides(probability), pad_sides(adjoint))
    return probability, adjoint, grad_conduct
```

```python
import functools

import jax
import jax.numpy as jnp
from jax import lax
from jax.experimental import pallas as pl
from jax.experimental.pallas import tpu as pltpu
from jax.sharding import PartitionSpec as P

seed_pull = 4.0
screening = 0.05

MESH = pl.DeviceIdType.MESH
COND, START, COT, RES, IMG, ADJ = range(6)
LOW_Y, HIGH_Y, LOW_Z, HIGH_Z = range(4)


def kernel(
    ny, nz,
    cond_in, seeds_in, labels_in, start_in, cot_in,
    prob_out, adj_out, grad_out,
    fields, prob, adj, grad, seeds, labels,
    edge_y, edge_z, edge_x, rim_z, halo_z, face_z, gathered,
    load_sem, store_sem, send_sem, recv_sem, gsend_sem, grecv_sem,
):
    rows, cols, lanes = cond_in.shape
    n = ny * nz
    gy = lax.axis_index("gy")
    gz = lax.axis_index("gz")
    me = gy * nz + gz
    inputs = {COND: cond_in, START: start_in, COT: cot_in}

    loads = []
    body = pl.ds(1, rows)
    for i, (src, dst) in enumerate((
        (cond_in, fields.at[COND, body]),
        (start_in, fields.at[START, body]),
        (seeds_in, seeds),
        (labels_in, labels),
        (cot_in, fields.at[COT, body]),
    )):
        copy = pltpu.make_async_copy(src, dst, load_sem.at[i])
        copy.start()
        loads.append(copy)

    barrier = pltpu.get_barrier_semaphore()
    for k in range(1, n):
        peer = lax.rem(me + k, n)
        pl.semaphore_signal(
            barrier, inc=1, device_id=(peer // nz, lax.rem(peer, nz)), device_id_type=MESH
        )

    has_low_y, has_high_y = gy > 0, gy < ny - 1
    has_low_z, has_high_z = gz > 0, gz < nz - 1
    can_send = (has_low_y, has_high_y, has_low_z, has_high_z)
    can_recv = (has_high_y, has_low_y, has_high_z, has_low_z)
    target = ((gy - 1, gz), (gy + 1, gz), (gy, gz - 1), (gy, gz + 1))

    def exchange(k, side):
        if side == LOW_Y:
            src = inputs[k].at[0] if k in inputs else fields.at[k, 1]
            dst = fields.at[k, rows + 1]
        elif side == HIGH_Y:
            src = inputs[k].at[rows - 1] if k in inputs else fields.at[k, rows]
            dst = fields.at[k, 0]
        elif side == LOW_Z:
            src = face_z.at[k, 0]
            dst = halo_z.at[k, 1]
        else:
            src = face_z.at[k, 1]
            dst = halo_z.at[k, 0]
        return pltpu.make_async_remote_copy(
            src_ref=src, dst_ref=dst, send_sem=send_sem.at[k, side],
            recv_sem=recv_sem.at[k, side], device_id=target[side], device_id_type=MESH,
        )

    def send(k, sides):
        for side in sides:
            @pl.when(can_send[side])
            def _():
                exchange(k, side).start()

    def arrive(k, sides):
        for side in sides:
            @pl.when(can_recv[side])
            def _():
                exchange(k, side).wait_recv()

    every = (LOW_Y, HIGH_Y, LOW_Z, HIGH_Z)

    def put_faces(k):
        face_z[k, 0] = fields[k, 1:rows + 1, 0:1, :]
        face_z[k, 1] = fields[k, 1:rows + 1, cols - 1:cols, :]

    plane = jnp.zeros((cols, lanes), jnp.float32)
    line = jnp.zeros((rows, 1, lanes), jnp.float32)
    for k in range(6):
        @pl.when(gy == 0)
        def _():
            fields[k, 0] = plane

        @pl.when(gy == ny - 1)
        def _():
            fields[k, rows + 1] = plane

        @pl.when(gz == 0)
        def _():
            halo_z[k, 0] = line

        @pl.when(gz == nz - 1)
        def _():
            halo_z[k, 1] = line

    loads[0].wait()
    put_faces(COND)
    loads[1].wait()
    put_faces(START)
    loads[4].wait()
    put_faces(COT)
    pl.semaphore_wait(barrier, n - 1)
    send(COND, every)
    send(START, every)
    send(COT, every)

    lane = lax.broadcasted_iota(jnp.int32, (cols, lanes), 1)
    col = lax.broadcasted_iota(jnp.int32, (cols, lanes), 0)

    def low_x(value):
        return pltpu.roll(value, 1, 1)

    def high_x(value):
        return pltpu.roll(value, lanes - 1, 1)

    def low_z(value):
        return pltpu.roll(value, 1, 0)

    def high_z(value):
        return pltpu.roll(value, cols - 1, 0)

    def weigh(low, high, keep):
        inverse = 1.0 / (low + high)
        if keep is not None:
            inverse = jnp.where(keep, inverse, 0.0)
        p = low * inverse
        q = high * inverse
        return 2.0 * high * p, 2.0 * p * p, 2.0 * q * q

    def put_edge(ref, at, parts):
        for i in range(3):
            ref[(i,) + at] = parts[i]

    def edge_step(y, carry):
        c = fields[COND, y + 1]
        put_edge(edge_x, (y,), weigh(low_x(c), c, lane > 0))
        put_edge(edge_z, (y,), weigh(low_z(c), c, col > 0))

        return carry

    def edge_y_step(y, carry):
        put_edge(edge_y, (y,), weigh(fields[COND, y], fields[COND, y + 1], None))
        return carry

    lax.fori_loop(0, rows, edge_step, 0)
    lax.fori_loop(1, rows, edge_y_step, 0)
    edge_y[0, 0] = plane
    edge_y[0, rows] = plane
    loads[2].wait()
    loads[3].wait()

    def inner_plane(k, y):
        f = fields[k, y + 1]
        pull = seed_pull * seeds[y].astype(jnp.float32) + screening
        fx = edge_x[0, y] * (f - low_x(f))
        fz = edge_z[0, y] * (f - low_z(f))
        out = pull * f + (fx - high_x(fx)) + (fz - high_z(fz))
        if not (isinstance(y, int) and y == 0):
            out = out + edge_y[0, y] * (f - fields[k, y])
        if not (isinstance(y, int) and y == rows - 1):
            out = out - edge_y[0, y + 1] * (fields[k, y + 2] - f)
        return out

    def image(k, put):
        put(0, inner_plane(k, 0))

        def step(y, carry):
            put(y, inner_plane(k, y))
            return carry

        lax.fori_loop(1, rows - 1, step, 0)
        put(rows - 1, inner_plane(k, rows - 1))

    def rim(k, out, sign):
        low = rim_z[0, 0] * (fields[k, 1:rows + 1, 0:1, :] - halo_z[k, 0])
        high = rim_z[0, 1] * (fields[k, 1:rows + 1, cols - 1:cols, :] - halo_z[k, 1])
        fields[out, 1:rows + 1, 0:1, :] = fields[out, 1:rows + 1, 0:1, :] + sign * low
        fields[out, 1:rows + 1, cols - 1:cols, :] = (
            fields[out, 1:rows + 1, cols - 1:cols, :] + sign * high
        )
        low = edge_y[0, 0] * (fields[k, 1] - fields[k, 0])
        high = edge_y[0, rows] * (fields[k, rows] - fields[k, rows + 1])
        fields[out, 1] = fields[out, 1] + sign * low
        fields[out, rows] = fields[out, rows] + sign * high

    def put_residual(y, value):
        rhs = seed_pull * (seeds[y] * labels[y]).astype(jnp.float32)
        fields[RES, y + 1] = rhs - value

    def put_image(out):
        def put(y, value):
            fields[out, y + 1] = value

        return put

    image(START, put_residual)
    image(COT, put_image(ADJ))

    arrive(COND, every)
    put_edge(edge_y, (0,), weigh(fields[COND, 0], fields[COND, 1], None))
    put_edge(edge_y, (rows,), weigh(fields[COND, rows], fields[COND, rows + 1], None))
    put_edge(rim_z, (0,), weigh(halo_z[COND, 0], fields[COND, 1:rows + 1, 0:1, :], None))
    put_edge(
        rim_z, (1,), weigh(fields[COND, 1:rows + 1, cols - 1:cols, :], halo_z[COND, 1], None)
    )
    arrive(START, every)
    rim(START, RES, -1.0)
    put_faces(RES)
    send(RES, every)
    image(RES, put_image(IMG))

    arrive(COT, every)
    rim(COT, ADJ, 1.0)
    put_faces(ADJ)

    arrive(RES, every)
    rim(RES, IMG, 1.0)
    put_faces(IMG)
    send(IMG, (HIGH_Y, HIGH_Z))
    send(ADJ, (HIGH_Y, HIGH_Z))
    send(IMG, (LOW_Y, LOW_Z))
    send(ADJ, (LOW_Y, LOW_Z))

    def fold(value):
        return jnp.sum(value.reshape(cols // 8, 8, lanes), axis=0)

    zero8 = jnp.zeros((8, lanes), jnp.float32)

    def total(value):
        return jnp.sum(jnp.sum(value, axis=0, keepdims=True), axis=1, keepdims=True)

    def shift_of(k, out):
        def step(y, carry):
            norm, product = carry
            f = fields[k, y + 1]
            return norm + fold(f * f), product + fold(f * fields[out, y + 1])

        norm, product = lax.fori_loop(0, rows, step, (zero8, zero8))
        return total(product) / jnp.maximum(total(norm), 1e-30)

    def moments(k, out, shift):
        def edge_sums(weight, df, dg):
            wf = weight * df
            wg = weight * dg
            return wf * df, wf * dg, wg * dg

        def step(y, carry):
            f = fields[k, y + 1]
            g = fields[out, y + 1] - shift * f
            pull = seed_pull * seeds[y].astype(jnp.float32) + screening
            f2, fg, g2 = f * f, f * g, g * g
            sums = [pull * f2, pull * fg, pull * g2]
            for weight, lower in ((edge_x[0, y], low_x), (edge_z[0, y], low_z)):
                more = edge_sums(weight, f - lower(f), g - lower(g))
                sums = [a + b for a, b in zip(sums, more)]
            fb = fields[k, y]
            gb = fields[out, y] - shift * fb
            keep = jnp.where(y > 0, 1.0, 0.0)
            more = edge_sums(edge_y[0, y] * keep, f - fb, g - gb)
            sums = [a + b for a, b in zip(sums, more)]
            return tuple(c + fold(v) for c, v in zip(carry, [f2, fg, g2] + sums))

        first = step_first(k, out, shift, edge_sums)
        return list(lax.fori_loop(1, rows, step, first))

    def step_first(k, out, shift, edge_sums):
        f = fields[k, 1]
        g = fields[out, 1] - shift * f
        pull = seed_pull * seeds[0].astype(jnp.float32) + screening
        f2, fg, g2 = f * f, f * g, g * g
        sums = [pull * f2, pull * fg, pull * g2]
        for weight, lower in ((edge_x[0, 0], low_x), (edge_z[0, 0], low_z)):
            more = edge_sums(weight, f - lower(f), g - lower(g))
            sums = [a + b for a, b in zip(sums, more)]
        return tuple(fold(v) for v in [f2, fg, g2] + sums)

    def rim_moments(k, out, shift, sums):
        fb, fc = fields[k, 0], fields[k, 1]
        df = fc - fb
        dg = (fields[out, 1] - fields[out, 0]) - shift * df
        wf, wg = edge_y[0, 0] * df, edge_y[0, 0] * dg
        more = [fold(v) for v in (wf * df, wf * dg, wg * dg)]
        df = fields[k, 1:rows + 1, 0:1, :] - halo_z[k, 0]
        dg = (fields[out, 1:rows + 1, 0:1, :] - halo_z[out, 0]) - shift[None] * df
        wf, wg = rim_z[0, 0] * df, rim_z[0, 0] * dg
        lines = [jnp.sum(v, axis=0) for v in (wf * df, wf * dg, wg * dg)]
        ends = sums[:3]
        for a, b, c in zip(sums[3:], more, lines):
            ends.append(jnp.sum(a + b, axis=0, keepdims=True) + c)
        return [jnp.sum(v, axis=0, keepdims=True) for v in ends[:3]] + ends[3:]

    shift_r = shift_of(RES, IMG)
    sums_r = moments(RES, IMG, shift_r)
    shift_a = shift_of(COT, ADJ)
    sums_a = moments(COT, ADJ, shift_a)
    arrive(ADJ, (HIGH_Y, HIGH_Z))
    sums_a = rim_moments(COT, ADJ, shift_a, sums_a)
    arrive(IMG, (HIGH_Y, HIGH_Z))
    sums_r = rim_moments(RES, IMG, shift_r, sums_r)

    row16 = lax.broadcasted_iota(jnp.int32, (16, lanes), 0)
    lane16 = lax.broadcasted_iota(jnp.int32, (16, lanes), 1)
    stack = jnp.zeros((16, lanes), jnp.float32)
    for base, sums in ((0, sums_r), (8, sums_a)):
        for i, value in enumerate(sums):
            stack = jnp.where(row16 == base + i, value, stack)
    stack = jnp.sum(stack, axis=1, keepdims=True)
    stack = jnp.where(row16 == 6, shift_r, stack)
    stack = jnp.where(row16 == 14, shift_a, stack)
    gathered[me] = jnp.sum(jnp.where(row16 == lane16, stack, 0.0), axis=0, keepdims=True)

    def share(k, slot):
        peer = lax.rem(me + k, n)
        return pltpu.make_async_remote_copy(
            src_ref=gathered.at[slot], dst_ref=gathered.at[slot], send_sem=gsend_sem.at[k],
            recv_sem=grecv_sem.at[k], device_id=(peer // nz, lax.rem(peer, nz)),
            device_id_type=MESH,
        )

    for k in range(1, n):
        share(k, me).start()
    arrive(IMG, (LOW_Y, LOW_Z))
    arrive(ADJ, (LOW_Y, LOW_Z))
    for k in range(1, n):
        share(k, lax.rem(me + n - k, n)).wait_recv()

    g = gathered[...].reshape(n, lanes)

    def at_shift(value, i):
        return pltpu.roll(value, 6 - i, 1)

    norm = jnp.sum(at_shift(g, 0), axis=0, keepdims=True)
    energy = jnp.sum(at_shift(g, 3), axis=0, keepdims=True)
    delta = g - energy / norm
    residual = at_shift(g, 2) + delta * (2.0 * at_shift(g, 1) + delta * at_shift(g, 0))
    product = at_shift(g, 5) + delta * (2.0 * at_shift(g, 4) + delta * at_shift(g, 3))
    alpha = norm / energy
    norm_next = alpha * alpha * jnp.sum(residual, axis=0, keepdims=True)
    product = alpha * alpha * jnp.sum(product, axis=0, keepdims=True)
    ratio = norm_next / norm
    curve = product - ratio * norm_next / alpha
    alpha_next = jnp.where(curve > 0.0, norm_next / curve, 0.0)
    on_res = alpha + alpha_next * (1.0 + ratio)
    on_img = -alpha * alpha_next
    one = lax.broadcasted_iota(jnp.int32, (1, lanes), 1)

    def pick(value, i):
        return jnp.sum(jnp.where(one == i, value, 0.0), axis=1, keepdims=True)

    res_r, img_r = pick(on_res, 6), pick(on_img, 6)
    res_a, img_a = pick(on_res, 14), pick(on_img, 14)

    def final_step(y, carry):
        prob[y] = fields[START, y] + res_r * fields[RES, y] + img_r * fields[IMG, y]
        adj[y] = res_a * fields[COT, y] + img_a * fields[ADJ, y]
        return carry

    lax.fori_loop(0, rows + 2, final_step, 0)
    stores = [
        pltpu.make_async_copy(prob.at[body], prob_out, store_sem.at[0]),
        pltpu.make_async_copy(adj.at[body], adj_out, store_sem.at[1]),
    ]
    for copy in stores:
        copy.start()

    def grad_step(y, carry):
        u, v = prob[y + 1], adj[y + 1]
        d = (u - low_x(u)) * (v - low_x(v))
        out = edge_x[1, y] * d + high_x(edge_x[2, y] * d)
        d = (u - low_z(u)) * (v - low_z(v))
        out = out + edge_z[1, y] * d + high_z(edge_z[2, y] * d)
        out = out + edge_y[1, y] * ((u - prob[y]) * (v - adj[y]))
        out = out + edge_y[2, y + 1] * ((u - prob[y + 2]) * (v - adj[y + 2]))
        grad[y] = -out
        return carry

    lax.fori_loop(0, rows, grad_step, 0)
    for side, at, part in ((0, 0, 1), (1, cols - 1, 2)):
        beside = pl.ds(at, 1)
        u = halo_z[START, side] + res_r[None] * halo_z[RES, side] + img_r[None] * halo_z[IMG, side]
        v = res_a[None] * halo_z[COT, side] + img_a[None] * halo_z[ADJ, side]
        du = prob[1:rows + 1, beside, :] - u
        dv = adj[1:rows + 1, beside, :] - v
        grad[:, beside, :] = grad[:, beside, :] - rim_z[part, side] * (du * dv)
    copy = pltpu.make_async_copy(grad, grad_out, store_sem.at[2])
    copy.start()
    stores.append(copy)

    for k in range(6):
        for side in every:
            @pl.when(can_send[side])
            def _():
                exchange(k, side).wait_send()
    for k in range(1, n):
        share(k, me).wait_send()
    for copy in stores:
        copy.wait()


def per_device(ny, nz, conduct, seeds, labels, start, cotangent):
    rows, cols, lanes = conduct.shape
    n = ny * nz
    block = jax.ShapeDtypeStruct(conduct.shape, jnp.float32)
    f32 = jnp.float32
    return pl.pallas_call(
        functools.partial(kernel, ny, nz),
        out_shape=(block, block, block),
        in_specs=[pl.BlockSpec(memory_space=pl.ANY)] * 5,
        out_specs=[pl.BlockSpec(memory_space=pl.ANY)] * 3,
        scratch_shapes=[
            pltpu.VMEM((6, rows + 2, cols, lanes), f32),
            pltpu.VMEM((rows + 2, cols, lanes), f32),
            pltpu.VMEM((rows + 2, cols, lanes), f32),
            pltpu.VMEM((rows, cols, lanes), f32),
            pltpu.VMEM((rows, cols, lanes), jnp.int32),
            pltpu.VMEM((rows, cols, lanes), jnp.int32),
            pltpu.VMEM((3, rows + 1, cols, lanes), f32),
            pltpu.VMEM((3, rows, cols, lanes), f32),
            pltpu.VMEM((3, rows, cols, lanes), f32),
            pltpu.VMEM((3, 2, rows, 1, lanes), f32),
            pltpu.VMEM((6, 2, rows, 1, lanes), f32),
            pltpu.VMEM((6, 2, rows, 1, lanes), f32),
            pltpu.VMEM((n, 1, lanes), f32),
            pltpu.SemaphoreType.DMA((5,)),
            pltpu.SemaphoreType.DMA((3,)),
            pltpu.SemaphoreType.DMA((6, 4)),
            pltpu.SemaphoreType.DMA((6, 4)),
            pltpu.SemaphoreType.DMA((n,)),
            pltpu.SemaphoreType.DMA((n,)),
        ],
        compiler_params=pltpu.CompilerParams(collective_id=0, has_side_effects=True),
    )(conduct, seeds, labels, start, cotangent)


def solution(mesh):
    ny, nz = mesh.shape["gy"], mesh.shape["gz"]
    spec = P("gy", "gz", None)
    return jax.shard_map(
        functools.partial(per_device, ny, nz),
        mesh=mesh, in_specs=(spec,) * 5, out_specs=(spec,) * 3, check_vma=False,
    )
```

```python
import functools

import jax
import jax.numpy as jnp
from jax import lax
from jax.experimental import pallas as pl
from jax.experimental.pallas import tpu as pltpu
from jax.sharding import PartitionSpec as P

seed_pull = 4.0
screening = 0.05

MESH = pl.DeviceIdType.MESH
COND, START, COT, RES, IMG, ADJ = range(6)
LOW_Y, HIGH_Y, LOW_Z, HIGH_Z = range(4)


UNROLL = 4


def loop(low, high, step, carry):
    whole = (high - low) // UNROLL

    def block(i, carry):
        for j in range(UNROLL):
            carry = step(low + i * UNROLL + j, carry)
        return carry

    if whole > 1:
        carry = lax.fori_loop(0, whole, block, carry)
        low = low + whole * UNROLL
    for y in range(low, high):
        carry = step(y, carry)
    return carry


def kernel(
    ny, nz,
    cond_in, seeds_in, labels_in, start_in, cot_in,
    prob_out, adj_out, grad_out,
    fields, prob, adj, grad, seeds, labels,
    edge_y, edge_z, edge_x, rim_z, halo_z, face_z, gathered,
    load_sem, store_sem, send_sem, recv_sem, gsend_sem, grecv_sem,
):
    rows, cols, lanes = cond_in.shape
    n = ny * nz
    gy = lax.axis_index("gy")
    gz = lax.axis_index("gz")
    me = gy * nz + gz
    inputs = {COND: cond_in, START: start_in, COT: cot_in}

    loads = []
    body = pl.ds(1, rows)
    for i, (src, dst) in enumerate((
        (cond_in, fields.at[COND, body]),
        (start_in, fields.at[START, body]),
        (seeds_in, seeds),
        (labels_in, labels),
        (cot_in, fields.at[COT, body]),
    )):
        copy = pltpu.make_async_copy(src, dst, load_sem.at[i])
        copy.start()
        loads.append(copy)

    def turn(position, step, size):
        moved = position + step
        return jnp.where(moved >= size, moved - size, moved)

    def peer(k):
        return turn(gy, k // nz, ny), turn(gz, k % nz, nz)

    def slot_from(k):
        return turn(gy, ny - k // nz, ny) * nz + turn(gz, nz - k % nz, nz)

    barrier = pltpu.get_barrier_semaphore()
    for k in range(1, n):
        pl.semaphore_signal(barrier, inc=1, device_id=peer(k), device_id_type=MESH)

    has_low_y, has_high_y = gy > 0, gy < ny - 1
    has_low_z, has_high_z = gz > 0, gz < nz - 1
    can_send = (has_low_y, has_high_y, has_low_z, has_high_z)
    can_recv = (has_high_y, has_low_y, has_high_z, has_low_z)
    target = ((gy - 1, gz), (gy + 1, gz), (gy, gz - 1), (gy, gz + 1))

    def exchange(k, side):
        if side == LOW_Y:
            src = inputs[k].at[0] if k in inputs else fields.at[k, 1]
            dst = fields.at[k, rows + 1]
        elif side == HIGH_Y:
            src = inputs[k].at[rows - 1] if k in inputs else fields.at[k, rows]
            dst = fields.at[k, 0]
        elif side == LOW_Z:
            src = face_z.at[k, 0]
            dst = halo_z.at[k, 1]
        else:
            src = face_z.at[k, 1]
            dst = halo_z.at[k, 0]
        return pltpu.make_async_remote_copy(
            src_ref=src, dst_ref=dst, send_sem=send_sem.at[k, side],
            recv_sem=recv_sem.at[k, side], device_id=target[side], device_id_type=MESH,
        )

    def send(k, sides):
        for side in sides:
            @pl.when(can_send[side])
            def _():
                exchange(k, side).start()

    def arrive(k, sides):
        for side in sides:
            @pl.when(can_recv[side])
            def _():
                exchange(k, side).wait_recv()

    every = (LOW_Y, HIGH_Y, LOW_Z, HIGH_Z)

    def put_faces(k):
        face_z[k, 0] = fields[k, 1:rows + 1, 0:1, :]
        face_z[k, 1] = fields[k, 1:rows + 1, cols - 1:cols, :]

    plane = jnp.zeros((cols, lanes), jnp.float32)
    line = jnp.zeros((rows, 1, lanes), jnp.float32)
    for k in range(6):
        @pl.when(gy == 0)
        def _():
            fields[k, 0] = plane

        @pl.when(gy == ny - 1)
        def _():
            fields[k, rows + 1] = plane

        @pl.when(gz == 0)
        def _():
            halo_z[k, 0] = line

        @pl.when(gz == nz - 1)
        def _():
            halo_z[k, 1] = line

    loads[0].wait()
    put_faces(COND)
    loads[1].wait()
    put_faces(START)
    loads[4].wait()
    put_faces(COT)
    pl.semaphore_wait(barrier, n - 1)
    send(COND, every)
    send(START, every)
    send(COT, every)

    lane = lax.broadcasted_iota(jnp.int32, (cols, lanes), 1)
    col = lax.broadcasted_iota(jnp.int32, (cols, lanes), 0)

    def low_x(value):
        return pltpu.roll(value, 1, 1)

    def high_x(value):
        return pltpu.roll(value, lanes - 1, 1)

    def low_z(value):
        return pltpu.roll(value, 1, 0)

    def high_z(value):
        return pltpu.roll(value, cols - 1, 0)

    def weigh(low, high, keep):
        inverse = 1.0 / (low + high)
        if keep is not None:
            inverse = jnp.where(keep, inverse, 0.0)
        p = low * inverse
        q = high * inverse
        return 2.0 * high * p, 2.0 * p * p, 2.0 * q * q

    def put_edge(ref, at, parts):
        for i in range(3):
            ref[(i,) + at] = parts[i]

    def edge_step(y, carry):
        c = fields[COND, y + 1]
        put_edge(edge_x, (y,), weigh(low_x(c), c, lane > 0))
        put_edge(edge_z, (y,), weigh(low_z(c), c, col > 0))

        return carry

    def edge_y_step(y, carry):
        put_edge(edge_y, (y,), weigh(fields[COND, y], fields[COND, y + 1], None))
        return carry

    loop(0, rows, edge_step, 0)
    loop(1, rows, edge_y_step, 0)
    edge_y[0, 0] = plane
    edge_y[0, rows] = plane
    loads[2].wait()
    loads[3].wait()

    def inner_plane(k, y):
        f = fields[k, y + 1]
        pull = seed_pull * seeds[y].astype(jnp.float32) + screening
        fx = edge_x[0, y] * (f - low_x(f))
        fz = edge_z[0, y] * (f - low_z(f))
        out = pull * f + (fx - high_x(fx)) + (fz - high_z(fz))
        if not (isinstance(y, int) and y == 0):
            out = out + edge_y[0, y] * (f - fields[k, y])
        if not (isinstance(y, int) and y == rows - 1):
            out = out - edge_y[0, y + 1] * (fields[k, y + 2] - f)
        return out

    def image(k, put):
        put(0, inner_plane(k, 0))

        def step(y, carry):
            put(y, inner_plane(k, y))
            return carry

        loop(1, rows - 1, step, 0)
        put(rows - 1, inner_plane(k, rows - 1))

    def rim(k, out, sign):
        low = rim_z[0, 0] * (fields[k, 1:rows + 1, 0:1, :] - halo_z[k, 0])
        high = rim_z[0, 1] * (fields[k, 1:rows + 1, cols - 1:cols, :] - halo_z[k, 1])
        fields[out, 1:rows + 1, 0:1, :] = fields[out, 1:rows + 1, 0:1, :] + sign * low
        fields[out, 1:rows + 1, cols - 1:cols, :] = (
            fields[out, 1:rows + 1, cols - 1:cols, :] + sign * high
        )
        low = edge_y[0, 0] * (fields[k, 1] - fields[k, 0])
        high = edge_y[0, rows] * (fields[k, rows] - fields[k, rows + 1])
        fields[out, 1] = fields[out, 1] + sign * low
        fields[out, rows] = fields[out, rows] + sign * high

    def put_residual(y, value):
        rhs = seed_pull * (seeds[y] * labels[y]).astype(jnp.float32)
        fields[RES, y + 1] = rhs - value

    def put_image(out):
        def put(y, value):
            fields[out, y + 1] = value

        return put

    image(START, put_residual)
    image(COT, put_image(ADJ))

    arrive(COND, every)
    put_edge(edge_y, (0,), weigh(fields[COND, 0], fields[COND, 1], None))
    put_edge(edge_y, (rows,), weigh(fields[COND, rows], fields[COND, rows + 1], None))
    put_edge(rim_z, (0,), weigh(halo_z[COND, 0], fields[COND, 1:rows + 1, 0:1, :], None))
    put_edge(
        rim_z, (1,), weigh(fields[COND, 1:rows + 1, cols - 1:cols, :], halo_z[COND, 1], None)
    )
    arrive(START, every)
    rim(START, RES, -1.0)
    put_faces(RES)
    send(RES, every)
    image(RES, put_image(IMG))

    arrive(COT, every)
    rim(COT, ADJ, 1.0)
    put_faces(ADJ)

    arrive(RES, every)
    rim(RES, IMG, 1.0)
    put_faces(IMG)
    send(IMG, (HIGH_Y, HIGH_Z))
    send(ADJ, (HIGH_Y, HIGH_Z))
    send(IMG, (LOW_Y, LOW_Z))
    send(ADJ, (LOW_Y, LOW_Z))

    def fold(value):
        return jnp.sum(value.reshape(cols // 8, 8, lanes), axis=0)

    zero8 = jnp.zeros((8, lanes), jnp.float32)

    def total(value):
        return jnp.sum(jnp.sum(value, axis=0, keepdims=True), axis=1, keepdims=True)

    def shift_of(k, out):
        def step(y, carry):
            norm, product = carry
            f = fields[k, y + 1]
            return norm + fold(f * f), product + fold(f * fields[out, y + 1])

        norm, product = loop(0, rows, step, (zero8, zero8))
        return total(product) / jnp.maximum(total(norm), 1e-30)

    def moments(k, out, shift):
        def edge_sums(weight, df, dg):
            wf = weight * df
            wg = weight * dg
            return wf * df, wf * dg, wg * dg

        def step(y, carry):
            f = fields[k, y + 1]
            g = fields[out, y + 1] - shift * f
            pull = seed_pull * seeds[y].astype(jnp.float32) + screening
            f2, fg, g2 = f * f, f * g, g * g
            sums = [pull * f2, pull * fg, pull * g2]
            for weight, lower in ((edge_x[0, y], low_x), (edge_z[0, y], low_z)):
                more = edge_sums(weight, f - lower(f), g - lower(g))
                sums = [a + b for a, b in zip(sums, more)]
            fb = fields[k, y]
            gb = fields[out, y] - shift * fb
            keep = jnp.where(y > 0, 1.0, 0.0)
            more = edge_sums(edge_y[0, y] * keep, f - fb, g - gb)
            sums = [a + b for a, b in zip(sums, more)]
            return tuple(c + fold(v) for c, v in zip(carry, [f2, fg, g2] + sums))

        first = step_first(k, out, shift, edge_sums)
        return list(loop(1, rows, step, first))

    def step_first(k, out, shift, edge_sums):
        f = fields[k, 1]
        g = fields[out, 1] - shift * f
        pull = seed_pull * seeds[0].astype(jnp.float32) + screening
        f2, fg, g2 = f * f, f * g, g * g
        sums = [pull * f2, pull * fg, pull * g2]
        for weight, lower in ((edge_x[0, 0], low_x), (edge_z[0, 0], low_z)):
            more = edge_sums(weight, f - lower(f), g - lower(g))
            sums = [a + b for a, b in zip(sums, more)]
        return tuple(fold(v) for v in [f2, fg, g2] + sums)

    def rim_moments(k, out, shift, sums):
        fb, fc = fields[k, 0], fields[k, 1]
        df = fc - fb
        dg = (fields[out, 1] - fields[out, 0]) - shift * df
        wf, wg = edge_y[0, 0] * df, edge_y[0, 0] * dg
        more = [fold(v) for v in (wf * df, wf * dg, wg * dg)]
        df = fields[k, 1:rows + 1, 0:1, :] - halo_z[k, 0]
        dg = (fields[out, 1:rows + 1, 0:1, :] - halo_z[out, 0]) - shift[None] * df
        wf, wg = rim_z[0, 0] * df, rim_z[0, 0] * dg
        lines = [jnp.sum(v, axis=0) for v in (wf * df, wf * dg, wg * dg)]
        ends = sums[:3]
        for a, b, c in zip(sums[3:], more, lines):
            ends.append(jnp.sum(a + b, axis=0, keepdims=True) + c)
        return [jnp.sum(v, axis=0, keepdims=True) for v in ends[:3]] + ends[3:]

    shift_r = shift_of(RES, IMG)
    sums_r = moments(RES, IMG, shift_r)
    shift_a = shift_of(COT, ADJ)
    sums_a = moments(COT, ADJ, shift_a)
    arrive(ADJ, (HIGH_Y, HIGH_Z))
    sums_a = rim_moments(COT, ADJ, shift_a, sums_a)
    arrive(IMG, (HIGH_Y, HIGH_Z))
    sums_r = rim_moments(RES, IMG, shift_r, sums_r)

    row16 = lax.broadcasted_iota(jnp.int32, (16, lanes), 0)
    lane16 = lax.broadcasted_iota(jnp.int32, (16, lanes), 1)
    stack = jnp.zeros((16, lanes), jnp.float32)
    for base, sums in ((0, sums_r), (8, sums_a)):
        for i, value in enumerate(sums):
            stack = jnp.where(row16 == base + i, value, stack)
    stack = jnp.sum(stack, axis=1, keepdims=True)
    stack = jnp.where(row16 == 6, shift_r, stack)
    stack = jnp.where(row16 == 14, shift_a, stack)
    gathered[me] = jnp.sum(jnp.where(row16 == lane16, stack, 0.0), axis=0, keepdims=True)

    def share(k, slot):
        return pltpu.make_async_remote_copy(
            src_ref=gathered.at[slot], dst_ref=gathered.at[slot], send_sem=gsend_sem.at[k],
            recv_sem=grecv_sem.at[k], device_id=peer(k),
            device_id_type=MESH,
        )

    for k in range(1, n):
        share(k, me).start()
    arrive(IMG, (LOW_Y, LOW_Z))
    arrive(ADJ, (LOW_Y, LOW_Z))
    for k in range(1, n):
        share(k, slot_from(k)).wait_recv()

    g = gathered[...].reshape(n, lanes)

    def at_shift(value, i):
        return pltpu.roll(value, 6 - i, 1)

    norm = jnp.sum(at_shift(g, 0), axis=0, keepdims=True)
    energy = jnp.sum(at_shift(g, 3), axis=0, keepdims=True)
    delta = g - energy / norm
    residual = at_shift(g, 2) + delta * (2.0 * at_shift(g, 1) + delta * at_shift(g, 0))
    product = at_shift(g, 5) + delta * (2.0 * at_shift(g, 4) + delta * at_shift(g, 3))
    alpha = norm / energy
    norm_next = alpha * alpha * jnp.sum(residual, axis=0, keepdims=True)
    product = alpha * alpha * jnp.sum(product, axis=0, keepdims=True)
    ratio = norm_next / norm
    curve = product - ratio * norm_next / alpha
    alpha_next = jnp.where(curve > 0.0, norm_next / curve, 0.0)
    on_res = alpha + alpha_next * (1.0 + ratio)
    on_img = -alpha * alpha_next
    one = lax.broadcasted_iota(jnp.int32, (1, lanes), 1)

    def pick(value, i):
        return jnp.sum(jnp.where(one == i, value, 0.0), axis=1, keepdims=True)

    res_r, img_r = pick(on_res, 6), pick(on_img, 6)
    res_a, img_a = pick(on_res, 14), pick(on_img, 14)

    def final_step(y, carry):
        prob[y] = fields[START, y] + res_r * fields[RES, y] + img_r * fields[IMG, y]
        adj[y] = res_a * fields[COT, y] + img_a * fields[ADJ, y]
        return carry

    loop(0, rows + 2, final_step, 0)
    stores = [
        pltpu.make_async_copy(prob.at[body], prob_out, store_sem.at[0]),
        pltpu.make_async_copy(adj.at[body], adj_out, store_sem.at[1]),
    ]
    for copy in stores:
        copy.start()

    def grad_step(y, carry):
        u, v = prob[y + 1], adj[y + 1]
        d = (u - low_x(u)) * (v - low_x(v))
        out = edge_x[1, y] * d + high_x(edge_x[2, y] * d)
        d = (u - low_z(u)) * (v - low_z(v))
        out = out + edge_z[1, y] * d + high_z(edge_z[2, y] * d)
        out = out + edge_y[1, y] * ((u - prob[y]) * (v - adj[y]))
        out = out + edge_y[2, y + 1] * ((u - prob[y + 2]) * (v - adj[y + 2]))
        grad[y] = -out
        return carry

    loop(0, rows, grad_step, 0)
    for side, at, part in ((0, 0, 1), (1, cols - 1, 2)):
        beside = pl.ds(at, 1)
        u = halo_z[START, side] + res_r[None] * halo_z[RES, side] + img_r[None] * halo_z[IMG, side]
        v = res_a[None] * halo_z[COT, side] + img_a[None] * halo_z[ADJ, side]
        du = prob[1:rows + 1, beside, :] - u
        dv = adj[1:rows + 1, beside, :] - v
        grad[:, beside, :] = grad[:, beside, :] - rim_z[part, side] * (du * dv)
    copy = pltpu.make_async_copy(grad, grad_out, store_sem.at[2])
    copy.start()
    stores.append(copy)

    for k in range(6):
        for side in every:
            @pl.when(can_send[side])
            def _():
                exchange(k, side).wait_send()
    for k in range(1, n):
        share(k, me).wait_send()
    for copy in stores:
        copy.wait()


def per_device(ny, nz, conduct, seeds, labels, start, cotangent):
    rows, cols, lanes = conduct.shape
    n = ny * nz
    block = jax.ShapeDtypeStruct(conduct.shape, jnp.float32)
    f32 = jnp.float32
    return pl.pallas_call(
        functools.partial(kernel, ny, nz),
        out_shape=(block, block, block),
        in_specs=[pl.BlockSpec(memory_space=pl.ANY)] * 5,
        out_specs=[pl.BlockSpec(memory_space=pl.ANY)] * 3,
        scratch_shapes=[
            pltpu.VMEM((6, rows + 2, cols, lanes), f32),
            pltpu.VMEM((rows + 2, cols, lanes), f32),
            pltpu.VMEM((rows + 2, cols, lanes), f32),
            pltpu.VMEM((rows, cols, lanes), f32),
            pltpu.VMEM((rows, cols, lanes), jnp.int32),
            pltpu.VMEM((rows, cols, lanes), jnp.int32),
            pltpu.VMEM((3, rows + 1, cols, lanes), f32),
            pltpu.VMEM((3, rows, cols, lanes), f32),
            pltpu.VMEM((3, rows, cols, lanes), f32),
            pltpu.VMEM((3, 2, rows, 1, lanes), f32),
            pltpu.VMEM((6, 2, rows, 1, lanes), f32),
            pltpu.VMEM((6, 2, rows, 1, lanes), f32),
            pltpu.VMEM((n, 1, lanes), f32),
            pltpu.SemaphoreType.DMA((5,)),
            pltpu.SemaphoreType.DMA((3,)),
            pltpu.SemaphoreType.DMA((6, 4)),
            pltpu.SemaphoreType.DMA((6, 4)),
            pltpu.SemaphoreType.DMA((n,)),
            pltpu.SemaphoreType.DMA((n,)),
        ],
        compiler_params=pltpu.CompilerParams(collective_id=0, has_side_effects=True),
    )(conduct, seeds, labels, start, cotangent)


def solution(mesh):
    ny, nz = mesh.shape["gy"], mesh.shape["gz"]
    spec = P("gy", "gz", None)
    return jax.shard_map(
        functools.partial(per_device, ny, nz),
        mesh=mesh, in_specs=(spec,) * 5, out_specs=(spec,) * 3, check_vma=False,
    )
```

```python
import functools

import jax
import jax.numpy as jnp
from jax import lax
from jax.experimental import pallas as pl
from jax.experimental.pallas import tpu as pltpu
from jax.sharding import PartitionSpec as P

seed_pull = 4.0
screening = 0.05

MESH = pl.DeviceIdType.MESH
COND, START, COT, RES, IMG, ADJ = range(6)
LOW_Y, HIGH_Y, LOW_Z, HIGH_Z = range(4)


UNROLL = 4


def loop(low, high, step, carry):
    whole = (high - low) // UNROLL

    def block(i, carry):
        for j in range(UNROLL):
            carry = step(low + i * UNROLL + j, carry)
        return carry

    if whole > 1:
        carry = lax.fori_loop(0, whole, block, carry)
        low = low + whole * UNROLL
    for y in range(low, high):
        carry = step(y, carry)
    return carry


def kernel(
    ny, nz,
    cond_in, seeds_in, labels_in, start_in, cot_in,
    prob, adj, grad,
    fields, seeds, labels,
    edge_y, edge_z, edge_x, rim_z, halo_z, face_z, gathered,
    load_sem, send_sem, recv_sem, gsend_sem, grecv_sem,
):
    rows, cols, lanes = cond_in.shape
    n = ny * nz
    gy = lax.axis_index("gy")
    gz = lax.axis_index("gz")
    me = gy * nz + gz
    inputs = {COND: cond_in, START: start_in, COT: cot_in}

    loads = []
    body = pl.ds(1, rows)
    for i, (src, dst) in enumerate((
        (cond_in, fields.at[COND, body]),
        (start_in, fields.at[START, body]),
        (seeds_in, seeds),
        (labels_in, labels),
        (cot_in, fields.at[COT, body]),
    )):
        copy = pltpu.make_async_copy(src, dst, load_sem.at[i])
        copy.start()
        loads.append(copy)

    def turn(position, step, size):
        moved = position + step
        return jnp.where(moved >= size, moved - size, moved)

    def peer(k):
        return turn(gy, k // nz, ny), turn(gz, k % nz, nz)

    def slot_from(k):
        return turn(gy, ny - k // nz, ny) * nz + turn(gz, nz - k % nz, nz)

    barrier = pltpu.get_barrier_semaphore()
    for k in range(1, n):
        pl.semaphore_signal(barrier, inc=1, device_id=peer(k), device_id_type=MESH)

    has_low_y, has_high_y = gy > 0, gy < ny - 1
    has_low_z, has_high_z = gz > 0, gz < nz - 1
    can_send = (has_low_y, has_high_y, has_low_z, has_high_z)
    can_recv = (has_high_y, has_low_y, has_high_z, has_low_z)
    target = ((gy - 1, gz), (gy + 1, gz), (gy, gz - 1), (gy, gz + 1))

    def exchange(k, side):
        if side == LOW_Y:
            src = inputs[k].at[0] if k in inputs else fields.at[k, 1]
            dst = fields.at[k, rows + 1]
        elif side == HIGH_Y:
            src = inputs[k].at[rows - 1] if k in inputs else fields.at[k, rows]
            dst = fields.at[k, 0]
        elif side == LOW_Z:
            src = face_z.at[k, 0]
            dst = halo_z.at[k, 1]
        else:
            src = face_z.at[k, 1]
            dst = halo_z.at[k, 0]
        return pltpu.make_async_remote_copy(
            src_ref=src, dst_ref=dst, send_sem=send_sem.at[k, side],
            recv_sem=recv_sem.at[k, side], device_id=target[side], device_id_type=MESH,
        )

    def send(k, sides):
        for side in sides:
            @pl.when(can_send[side])
            def _():
                exchange(k, side).start()

    def arrive(k, sides):
        for side in sides:
            @pl.when(can_recv[side])
            def _():
                exchange(k, side).wait_recv()

    every = (LOW_Y, HIGH_Y, LOW_Z, HIGH_Z)

    def put_faces(k):
        face_z[k, 0] = fields[k, 1:rows + 1, 0:1, :]
        face_z[k, 1] = fields[k, 1:rows + 1, cols - 1:cols, :]

    plane = jnp.zeros((cols, lanes), jnp.float32)
    line = jnp.zeros((rows, 1, lanes), jnp.float32)
    for k in range(6):
        @pl.when(gy == 0)
        def _():
            fields[k, 0] = plane

        @pl.when(gy == ny - 1)
        def _():
            fields[k, rows + 1] = plane

        @pl.when(gz == 0)
        def _():
            halo_z[k, 0] = line

        @pl.when(gz == nz - 1)
        def _():
            halo_z[k, 1] = line

    loads[0].wait()
    put_faces(COND)
    loads[1].wait()
    put_faces(START)
    loads[4].wait()
    put_faces(COT)
    pl.semaphore_wait(barrier, n - 1)
    send(COND, every)
    send(START, every)
    send(COT, every)

    lane = lax.broadcasted_iota(jnp.int32, (cols, lanes), 1)
    col = lax.broadcasted_iota(jnp.int32, (cols, lanes), 0)

    def low_x(value):
        return pltpu.roll(value, 1, 1)

    def high_x(value):
        return pltpu.roll(value, lanes - 1, 1)

    def low_z(value):
        return pltpu.roll(value, 1, 0)

    def high_z(value):
        return pltpu.roll(value, cols - 1, 0)

    def weigh(low, high, keep):
        inverse = 1.0 / (low + high)
        if keep is not None:
            inverse = jnp.where(keep, inverse, 0.0)
        p = low * inverse
        q = high * inverse
        return 2.0 * high * p, 2.0 * p * p, 2.0 * q * q

    def put_edge(ref, at, parts):
        for i in range(3):
            ref[(i,) + at] = parts[i]

    def edge_step(y, carry):
        c = fields[COND, y + 1]
        put_edge(edge_x, (y,), weigh(low_x(c), c, lane > 0))
        put_edge(edge_z, (y,), weigh(low_z(c), c, col > 0))

        return carry

    def edge_y_step(y, carry):
        put_edge(edge_y, (y,), weigh(fields[COND, y], fields[COND, y + 1], None))
        return carry

    loop(0, rows, edge_step, 0)
    loop(1, rows, edge_y_step, 0)
    edge_y[0, 0] = plane
    edge_y[0, rows] = plane
    loads[2].wait()
    loads[3].wait()

    def inner_plane(k, y):
        f = fields[k, y + 1]
        pull = seed_pull * seeds[y].astype(jnp.float32) + screening
        fx = edge_x[0, y] * (f - low_x(f))
        fz = edge_z[0, y] * (f - low_z(f))
        out = pull * f + (fx - high_x(fx)) + (fz - high_z(fz))
        if not (isinstance(y, int) and y == 0):
            out = out + edge_y[0, y] * (f - fields[k, y])
        if not (isinstance(y, int) and y == rows - 1):
            out = out - edge_y[0, y + 1] * (fields[k, y + 2] - f)
        return out

    def image(k, put):
        put(0, inner_plane(k, 0))

        def step(y, carry):
            put(y, inner_plane(k, y))
            return carry

        loop(1, rows - 1, step, 0)
        put(rows - 1, inner_plane(k, rows - 1))

    def rim(k, out, sign):
        low = rim_z[0, 0] * (fields[k, 1:rows + 1, 0:1, :] - halo_z[k, 0])
        high = rim_z[0, 1] * (fields[k, 1:rows + 1, cols - 1:cols, :] - halo_z[k, 1])
        fields[out, 1:rows + 1, 0:1, :] = fields[out, 1:rows + 1, 0:1, :] + sign * low
        fields[out, 1:rows + 1, cols - 1:cols, :] = (
            fields[out, 1:rows + 1, cols - 1:cols, :] + sign * high
        )
        low = edge_y[0, 0] * (fields[k, 1] - fields[k, 0])
        high = edge_y[0, rows] * (fields[k, rows] - fields[k, rows + 1])
        fields[out, 1] = fields[out, 1] + sign * low
        fields[out, rows] = fields[out, rows] + sign * high

    def put_residual(y, value):
        rhs = seed_pull * (seeds[y] * labels[y]).astype(jnp.float32)
        fields[RES, y + 1] = rhs - value

    def put_image(out):
        def put(y, value):
            fields[out, y + 1] = value

        return put

    image(START, put_residual)
    image(COT, put_image(ADJ))

    arrive(COND, every)
    put_edge(edge_y, (0,), weigh(fields[COND, 0], fields[COND, 1], None))
    put_edge(edge_y, (rows,), weigh(fields[COND, rows], fields[COND, rows + 1], None))
    put_edge(rim_z, (0,), weigh(halo_z[COND, 0], fields[COND, 1:rows + 1, 0:1, :], None))
    put_edge(
        rim_z, (1,), weigh(fields[COND, 1:rows + 1, cols - 1:cols, :], halo_z[COND, 1], None)
    )
    arrive(START, every)
    rim(START, RES, -1.0)
    put_faces(RES)
    send(RES, every)
    image(RES, put_image(IMG))

    arrive(COT, every)
    rim(COT, ADJ, 1.0)
    put_faces(ADJ)
    send(ADJ, every)

    def fold(value):
        return jnp.sum(value.reshape(cols // 8, 8, lanes), axis=0)

    zero8 = jnp.zeros((8, lanes), jnp.float32)

    def total(value):
        return jnp.sum(jnp.sum(value, axis=0, keepdims=True), axis=1, keepdims=True)

    def shift_of(k, out):
        def step(y, carry):
            norm, product = carry
            f = fields[k, y + 1]
            return norm + fold(f * f), product + fold(f * fields[out, y + 1])

        norm, product = loop(0, rows, step, (zero8, zero8))
        return total(product) / jnp.maximum(total(norm), 1e-30)

    def moments(k, out, shift):
        def edge_sums(weight, df, dg):
            wf = weight * df
            wg = weight * dg
            return wf * df, wf * dg, wg * dg

        def step(y, carry):
            f = fields[k, y + 1]
            g = fields[out, y + 1] - shift * f
            pull = seed_pull * seeds[y].astype(jnp.float32) + screening
            f2, fg, g2 = f * f, f * g, g * g
            sums = [pull * f2, pull * fg, pull * g2]
            for weight, lower in ((edge_x[0, y], low_x), (edge_z[0, y], low_z)):
                more = edge_sums(weight, f - lower(f), g - lower(g))
                sums = [a + b for a, b in zip(sums, more)]
            fb = fields[k, y]
            gb = fields[out, y] - shift * fb
            keep = jnp.where(y > 0, 1.0, 0.0)
            more = edge_sums(edge_y[0, y] * keep, f - fb, g - gb)
            sums = [a + b for a, b in zip(sums, more)]
            return tuple(c + fold(v) for c, v in zip(carry, [f2, fg, g2] + sums))

        first = step_first(k, out, shift, edge_sums)
        return list(loop(1, rows, step, first))

    def step_first(k, out, shift, edge_sums):
        f = fields[k, 1]
        g = fields[out, 1] - shift * f
        pull = seed_pull * seeds[0].astype(jnp.float32) + screening
        f2, fg, g2 = f * f, f * g, g * g
        sums = [pull * f2, pull * fg, pull * g2]
        for weight, lower in ((edge_x[0, 0], low_x), (edge_z[0, 0], low_z)):
            more = edge_sums(weight, f - lower(f), g - lower(g))
            sums = [a + b for a, b in zip(sums, more)]
        return tuple(fold(v) for v in [f2, fg, g2] + sums)

    def rim_moments(k, out, shift, sums):
        fb, fc = fields[k, 0], fields[k, 1]
        df = fc - fb
        dg = (fields[out, 1] - fields[out, 0]) - shift * df
        wf, wg = edge_y[0, 0] * df, edge_y[0, 0] * dg
        more = [fold(v) for v in (wf * df, wf * dg, wg * dg)]
        df = fields[k, 1:rows + 1, 0:1, :] - halo_z[k, 0]
        dg = (fields[out, 1:rows + 1, 0:1, :] - halo_z[out, 0]) - shift[None] * df
        wf, wg = rim_z[0, 0] * df, rim_z[0, 0] * dg
        lines = [jnp.sum(v, axis=0) for v in (wf * df, wf * dg, wg * dg)]
        ends = sums[:3]
        for a, b, c in zip(sums[3:], more, lines):
            ends.append(jnp.sum(a + b, axis=0, keepdims=True) + c)
        return [jnp.sum(v, axis=0, keepdims=True) for v in ends[:3]] + ends[3:]

    shift_a = shift_of(COT, ADJ)
    sums_a = moments(COT, ADJ, shift_a)
    arrive(RES, every)
    rim(RES, IMG, 1.0)
    put_faces(IMG)
    send(IMG, (HIGH_Y, HIGH_Z))
    send(IMG, (LOW_Y, LOW_Z))

    shift_r = shift_of(RES, IMG)
    sums_r = moments(RES, IMG, shift_r)
    arrive(ADJ, (HIGH_Y, HIGH_Z))
    sums_a = rim_moments(COT, ADJ, shift_a, sums_a)
    arrive(IMG, (HIGH_Y, HIGH_Z))
    sums_r = rim_moments(RES, IMG, shift_r, sums_r)

    row16 = lax.broadcasted_iota(jnp.int32, (16, lanes), 0)
    lane16 = lax.broadcasted_iota(jnp.int32, (16, lanes), 1)
    stack = jnp.zeros((16, lanes), jnp.float32)
    for base, sums in ((0, sums_r), (8, sums_a)):
        for i, value in enumerate(sums):
            stack = jnp.where(row16 == base + i, value, stack)
    stack = jnp.sum(stack, axis=1, keepdims=True)
    stack = jnp.where(row16 == 6, shift_r, stack)
    stack = jnp.where(row16 == 14, shift_a, stack)
    gathered[me] = jnp.sum(jnp.where(row16 == lane16, stack, 0.0), axis=0, keepdims=True)

    def share(k, slot):
        return pltpu.make_async_remote_copy(
            src_ref=gathered.at[slot], dst_ref=gathered.at[slot], send_sem=gsend_sem.at[k],
            recv_sem=grecv_sem.at[k], device_id=peer(k),
            device_id_type=MESH,
        )

    for k in range(1, n):
        share(k, me).start()
    arrive(IMG, (LOW_Y, LOW_Z))
    arrive(ADJ, (LOW_Y, LOW_Z))
    for k in range(1, n):
        share(k, slot_from(k)).wait_recv()

    g = gathered[...].reshape(n, lanes)

    def at_shift(value, i):
        return pltpu.roll(value, 6 - i, 1)

    norm = jnp.sum(at_shift(g, 0), axis=0, keepdims=True)
    energy = jnp.sum(at_shift(g, 3), axis=0, keepdims=True)
    delta = g - energy / norm
    residual = at_shift(g, 2) + delta * (2.0 * at_shift(g, 1) + delta * at_shift(g, 0))
    product = at_shift(g, 5) + delta * (2.0 * at_shift(g, 4) + delta * at_shift(g, 3))
    alpha = norm / energy
    norm_next = alpha * alpha * jnp.sum(residual, axis=0, keepdims=True)
    product = alpha * alpha * jnp.sum(product, axis=0, keepdims=True)
    ratio = norm_next / norm
    curve = product - ratio * norm_next / alpha
    alpha_next = jnp.where(curve > 0.0, norm_next / curve, 0.0)
    on_res = alpha + alpha_next * (1.0 + ratio)
    on_img = -alpha * alpha_next
    one = lax.broadcasted_iota(jnp.int32, (1, lanes), 1)

    def pick(value, i):
        return jnp.sum(jnp.where(one == i, value, 0.0), axis=1, keepdims=True)

    res_r, img_r = pick(on_res, 6), pick(on_img, 6)
    res_a, img_a = pick(on_res, 14), pick(on_img, 14)

    def final_step(y, carry):
        prob[y] = fields[START, y] + res_r * fields[RES, y] + img_r * fields[IMG, y]
        adj[y] = res_a * fields[COT, y] + img_a * fields[ADJ, y]
        return carry

    loop(0, rows + 2, final_step, 0)
    def grad_step(y, carry):
        u, v = prob[y + 1], adj[y + 1]
        d = (u - low_x(u)) * (v - low_x(v))
        out = edge_x[1, y] * d + high_x(edge_x[2, y] * d)
        d = (u - low_z(u)) * (v - low_z(v))
        out = out + edge_z[1, y] * d + high_z(edge_z[2, y] * d)
        out = out + edge_y[1, y] * ((u - prob[y]) * (v - adj[y]))
        out = out + edge_y[2, y + 1] * ((u - prob[y + 2]) * (v - adj[y + 2]))
        grad[y] = -out
        return carry

    loop(0, rows, grad_step, 0)
    for side, at, part in ((0, 0, 1), (1, cols - 1, 2)):
        beside = pl.ds(at, 1)
        u = halo_z[START, side] + res_r[None] * halo_z[RES, side] + img_r[None] * halo_z[IMG, side]
        v = res_a[None] * halo_z[COT, side] + img_a[None] * halo_z[ADJ, side]
        du = prob[1:rows + 1, beside, :] - u
        dv = adj[1:rows + 1, beside, :] - v
        grad[:, beside, :] = grad[:, beside, :] - rim_z[part, side] * (du * dv)

    for k in range(6):
        for side in every:
            @pl.when(can_send[side])
            def _():
                exchange(k, side).wait_send()
    for k in range(1, n):
        share(k, me).wait_send()


def put_out(prob, adj, grad, prob_out, adj_out, grad_out, sem):
    body = pl.ds(1, grad.shape[0])
    copies = [
        pltpu.make_async_copy(prob.at[body], prob_out, sem.at[0]),
        pltpu.make_async_copy(adj.at[body], adj_out, sem.at[1]),
        pltpu.make_async_copy(grad, grad_out, sem.at[2]),
    ]
    for copy in copies:
        copy.start()
    for copy in copies:
        copy.wait()


def per_device(ny, nz, conduct, seeds, labels, start, cotangent):
    rows, cols, lanes = conduct.shape
    n = ny * nz
    block = jax.ShapeDtypeStruct(conduct.shape, jnp.float32)
    f32 = jnp.float32
    padded = pltpu.VMEM((rows + 2, cols, lanes), f32)
    made = pl.pallas_call(
        functools.partial(kernel, ny, nz),
        out_shape=(padded, padded, pltpu.VMEM((rows, cols, lanes), f32)),
        in_specs=[pl.BlockSpec(memory_space=pl.ANY)] * 5,
        out_specs=[pl.BlockSpec(memory_space=pltpu.VMEM)] * 3,
        scratch_shapes=[
            pltpu.VMEM((6, rows + 2, cols, lanes), f32),
            pltpu.VMEM((rows, cols, lanes), jnp.int32),
            pltpu.VMEM((rows, cols, lanes), jnp.int32),
            pltpu.VMEM((3, rows + 1, cols, lanes), f32),
            pltpu.VMEM((3, rows, cols, lanes), f32),
            pltpu.VMEM((3, rows, cols, lanes), f32),
            pltpu.VMEM((3, 2, rows, 1, lanes), f32),
            pltpu.VMEM((6, 2, rows, 1, lanes), f32),
            pltpu.VMEM((6, 2, rows, 1, lanes), f32),
            pltpu.VMEM((n, 1, lanes), f32),
            pltpu.SemaphoreType.DMA((5,)),
            pltpu.SemaphoreType.DMA((6, 4)),
            pltpu.SemaphoreType.DMA((6, 4)),
            pltpu.SemaphoreType.DMA((n,)),
            pltpu.SemaphoreType.DMA((n,)),
        ],
        compiler_params=pltpu.CompilerParams(collective_id=0, has_side_effects=True),
    )(conduct, seeds, labels, start, cotangent)
    return pl.pallas_call(
        put_out,
        out_shape=(block, block, block),
        in_specs=[pl.BlockSpec(memory_space=pltpu.VMEM)] * 3,
        out_specs=[pl.BlockSpec(memory_space=pl.ANY)] * 3,
        scratch_shapes=[pltpu.SemaphoreType.DMA((3,))],
    )(*made)


def solution(mesh):
    ny, nz = mesh.shape["gy"], mesh.shape["gz"]
    spec = P("gy", "gz", None)
    return jax.shard_map(
        functools.partial(per_device, ny, nz),
        mesh=mesh, in_specs=(spec,) * 5, out_specs=(spec,) * 3, check_vma=False,
    )
```
